32 devices in a mesh: groups: 2 (over x), expert: 16 (over z, y, core).
Axes of the slice: x: 2, y: 2, z: 4, core: 2. Of those that a mesh axis runs over, the one named last changes fastest.
Arguments:
- residual: bfloat16 [4096, 3584], P(('groups', 'expert')), parts along dimension 0, may hold values from -24 to 24
- norm_gain: float32 [3584], replicated, may hold values from 0.25 to 1.75
- router: bfloat16 [3584, 4], replicated, may hold values from -0.09375 to 0.09375
- w_gate: bfloat16 [3584, 4096], P(None, 'expert'), may hold values from -0.09375 to 0.09375
- w_up: bfloat16 [3584, 4096], P(None, 'expert'), may hold values from -0.09375 to 0.09375
- w_down: bfloat16 [4096, 3584], P('expert'), may hold values from -0.1875 to 0.1875
- expert_ids: int32 [4096, 2], P(('groups', 'expert')), parts along dimension 0, may hold values from 0 to 3, all different within a row; in each aligned block of 128 rows (0 to 127, 128 to 255, ...) at most 96 rows name the same one
Outputs:
- layer_out: bfloat16 [4096, 3584], P(('groups', 'expert')), parts along dimension 0
The draws below stay inside these ranges and needn't reach their ends.
There are 2 independent parts, one for each index of `groups`. The reference program is written for one: setup_inputs(seed, part) draws one part's arguments, and reference() takes and returns one part's arrays. A program takes and returns all parts, laid end to end along the dimension named above; an argument that names none is the same for every part. Nothing has to cross between parts.
Inputs may be any that keep to these rules, and one draw needn't show every extreme that they name: `expert_ids`: each row names 2 different experts. Within the rows of one device no expert is named by more than 96 rows, and in every draw some device's rows name some expert exactly 96 times.
All inputs are finite; a program needn't handle non-finite values.
Results may differ from the reference program's by a relative error of at most 0.0054.
Values may be sent and summed in bfloat16 or wider, within the bound.
A program may use at most 128 MiB of HBM per device.

```python
import math
import jax
import jax.numpy as jnp
import numpy as np
from jax import lax

D = 3584
FF_E = 1024
SPAN = 4
TOP = 2
TOK_DEV = 128
HID = 256
EXPERTS = 4
TOKENS = 2048
CAP = 96
N_EXPERT = 16


def draw_residual(key, part):
    noise_key = jax.random.fold_in(key, 11)
    column_key = jax.random.fold_in(key, 12)
    row_key = jax.random.fold_in(key, 13)
    column_scale = jnp.exp(jax.random.uniform(column_key, (1, D), jnp.float32, math.log(0.3), math.log(3.0)))
    row_scale = jnp.exp(jax.random.uniform(row_key, (TOKENS, 1), jnp.float32, math.log(0.5), math.log(2.0)))
    base_values = jnp.clip(jax.random.normal(noise_key, (TOKENS, D), jnp.float32), -4.0, 4.0)
    return (base_values * column_scale * row_scale).astype(jnp.bfloat16)


def shard_levels(stream_key, extent, cuts, low, top_value):
    gain, own = 1.0, jax.random.fold_in(stream_key, 6)
    for axis_at, blocks in cuts:
        steps = jnp.exp(jax.random.uniform(jax.random.fold_in(own, axis_at), (blocks,), jnp.float32, low / len(cuts), top_value / len(cuts)))
        gain = gain * jnp.repeat(steps, extent[axis_at] // blocks).reshape([-1 if axis == axis_at else 1 for axis in range(len(extent))])
    return gain


def deal_out(rng, own, number, rows, amount, top, most, skew):
    sequence = jax.random.permutation(rng, amount)
    packed, usual = shares(amount, rows * top, most, skew, True), shares(amount, rows * top, most, skew, False)
    places = jnp.arange(amount)

    def named(tallies, rotation):
        used = int((tallies > 0).sum())
        fixed = max(1, used // 4)
        shifted = fixed + (places - fixed + rotation * (used - fixed)) % max(1, amount - fixed)
        return jnp.zeros((amount,), jnp.int32).at[sequence[jnp.where(places < fixed, places, shifted)]].set(jnp.asarray(tallies, jnp.int32))

    tallies = jnp.where(number % 4 == 0, named(packed, number // 4), named(usual, number - number // 4 - 1))
    mixed = jax.random.permutation(jax.random.fold_in(own, 3), amount)
    giver, receiver = mixed[0:amount // 2 * 2:2], mixed[1:amount // 2 * 2:2]
    margin = jnp.minimum(tallies[giver] - 1, most - tallies[receiver]) // 2
    margin = jnp.where((giver == sequence[0]) | (receiver == sequence[0]) | (tallies[receiver] == 0), 0, jnp.maximum(margin, 0))
    shifted = jax.random.randint(jax.random.fold_in(own, 4), (amount // 2,), 0, 1 << 20) % (margin + 1)
    tallies = tallies.at[giver].add(-shifted).at[receiver].add(shifted)
    items = jnp.searchsorted(jnp.cumsum(tallies), jnp.arange(rows * top), side="right").astype(jnp.int32)
    table = items.reshape(top, rows).T
    table = table[jax.random.permutation(jax.random.fold_in(own, 1), rows)]
    rotation = jax.random.randint(jax.random.fold_in(own, 2), (rows, 1), 0, top)
    return jnp.take_along_axis(table, (jnp.arange(top)[None, :] + rotation) % top, axis=1)


def shares(count, total, reach, slope, full):
    portions = [(1 << 20) // math.isqrt(rank ** slope) + 1 for rank in range(1, count + 1)]
    largest = reach if full else min(reach, max(-(-total // count), total * portions[0] // sum(portions)))
    least = 1 if total - largest >= count - 1 else 0
    counts, spare = [largest] + [least] * (count - 1), total - largest - least * (count - 1)
    while spare > 0:
        free = [i for i in range(1, count) if counts[i] < largest] or [i for i in range(1, count) if counts[i] < reach]
        mass, remaining = sum([portions[i] for i in free]), spare
        for i in free:
            addition = min(reach - counts[i], max(1, remaining * portions[i] // mass), spare)
            counts[i] = counts[i] + addition
            spare = spare - addition
    return np.array(counts)


def scatter_about(stream_key, dims, spread, most, cuts=(), held_as=jnp.bfloat16):
    result = spread * jax.random.normal(stream_key, dims, jnp.float32)
    if cuts:
        result = result * shard_levels(stream_key, dims, cuts, -0.22, 0.18)
    return jnp.clip(result, -most, most).astype(held_as)


def setup_inputs(seed: int = 0, part: int = 0) -> dict:
    keys = jax.random.split(jax.random.key(seed), 8)
    own_keys = jax.random.split(jax.random.fold_in(keys[7], part), 8)
    residual = draw_residual(jax.random.fold_in(jax.random.fold_in(keys[7], part), 71), part)
    norm_gain = jnp.clip(1.0 + 0.15 * jax.random.normal(keys[1], (D,), jnp.float32), 0.25, 1.75)
    router = scatter_about(keys[2], (D, EXPERTS), D ** -0.5, 0.09375)
    w_gate = scatter_about(keys[3], (D, EXPERTS * FF_E), D ** -0.5, 0.09375, ((1, 16),))
    w_up = scatter_about(keys[4], (D, EXPERTS * FF_E), D ** -0.5, 0.09375, ((1, 16),))
    w_down = scatter_about(keys[5], (EXPERTS * FF_E, D), FF_E ** -0.5, 0.1875, ((0, 16),))
    expert_ids_keys = jax.random.split(jax.random.fold_in(own_keys[6], 1), TOKENS // TOK_DEV)
    expert_ids_turns = jax.random.permutation(jax.random.fold_in(own_keys[6], 3), TOKENS // TOK_DEV)
    expert_ids = jax.vmap(lambda own, number: deal_out(jax.random.fold_in(own_keys[6], 2), own, number, TOK_DEV, EXPERTS, TOP, CAP, 2))(expert_ids_keys, expert_ids_turns).reshape((TOKENS, TOP))
    return dict(residual=residual, norm_gain=norm_gain, router=router, w_gate=w_gate, w_up=w_up, w_down=w_down, expert_ids=expert_ids)


route_scale = 2.5
norm_eps = 1e-06

def normalize(residual, norm_gain):
    residual_wide = residual.astype(jnp.float32)
    mean_square = lax.optimization_barrier(jnp.mean(residual_wide * residual_wide, axis=1, keepdims=True))
    normed = (residual_wide * lax.rsqrt(mean_square + norm_eps) * norm_gain).astype(jnp.bfloat16)
    return (residual_wide, normed)

def routing(normed, router, expert_ids):
    logits = jnp.dot(normed, router, preferred_element_type=jnp.float32)
    affinity = jax.nn.sigmoid(logits)
    picked = expert_ids[:, :, None] == lax.iota(jnp.int32, router.shape[1])[None, None, :]
    chosen = lax.optimization_barrier(jnp.sum(jnp.where(picked, affinity[:, None, :], 0.0), axis=2))
    gate_values = route_scale * chosen / lax.optimization_barrier(jnp.sum(chosen, axis=1, keepdims=True))
    return (picked, gate_values)

def slot_numbers(picked, block_rows):
    total_rows, top_count, expert_count = picked.shape
    flat_pick = picked.reshape(total_rows // block_rows, block_rows * top_count, expert_count).astype(jnp.int32)
    before = jnp.cumsum(flat_pick, axis=1) - flat_pick
    return lax.optimization_barrier(jnp.sum(before * flat_pick, axis=2)).reshape(total_rows, top_count)

def reference(residual, norm_gain, router, w_gate, w_up, w_down, expert_ids):
    residual_wide, normed = normalize(residual, norm_gain)
    picked, gate_values = routing(normed, router, expert_ids)
    slot_index = slot_numbers(picked, TOK_DEV)
    block_index = lax.iota(jnp.int32, TOKENS) // TOK_DEV
    position = (block_index[:, None] * CAP + slot_index).astype(jnp.int32)
    owner_row = jnp.broadcast_to(lax.iota(jnp.int32, TOKENS)[:, None], (TOKENS, TOP))
    row_table = jnp.zeros((EXPERTS, N_EXPERT * CAP), jnp.int32).at[expert_ids, position].set(owner_row)
    filled = jnp.zeros((EXPERTS, N_EXPERT * CAP), jnp.int32).at[expert_ids, position].set(1)

    def one_expert(accumulated, expert):
        routed_rows = jnp.take(normed, row_table[expert], axis=0)
        routed_rows = jnp.where(filled[expert][:, None] > 0, routed_rows, jnp.zeros_like(routed_rows))
        summed = jnp.zeros((N_EXPERT * CAP, D), jnp.float32)
        for member in range(SPAN):
            column_start = (expert * SPAN + member) * HID
            gate_proj = jnp.dot(routed_rows, lax.dynamic_slice_in_dim(w_gate, column_start, HID, 1), preferred_element_type=jnp.float32)
            up_proj = jnp.dot(routed_rows, lax.dynamic_slice_in_dim(w_up, column_start, HID, 1), preferred_element_type=jnp.float32)
            activated = (jax.nn.silu(gate_proj) * up_proj).astype(jnp.bfloat16)
            partial_value = jnp.dot(activated, lax.dynamic_slice_in_dim(w_down, column_start, HID, 0), preferred_element_type=jnp.float32).astype(jnp.bfloat16)
            partial_value = lax.optimization_barrier(partial_value)
            summed = summed + partial_value.astype(jnp.float32)
        for route_rank in range(TOP):
            weight = jnp.where(expert_ids[:, route_rank] == expert, gate_values[:, route_rank], 0.0)
            accumulated = accumulated + weight[:, None] * jnp.take(summed, position[:, route_rank], axis=0)
        return (accumulated, None)
    accumulated, unused = lax.scan(one_expert, jnp.zeros((TOKENS, D), jnp.float32), lax.iota(jnp.int32, EXPERTS))
    return (residual_wide + accumulated).astype(jnp.bfloat16)
```

```python
import functools

import jax
import jax.numpy as jnp
from jax import lax
from jax.experimental import pallas as pl
from jax.experimental.pallas import tpu as pltpu
from jax.sharding import PartitionSpec as P

route_scale = 2.5
norm_eps = 1e-06
LANES = 128
MESH = pl.DeviceIdType.MESH

TOK_PIECES = 2
OUT_PIECES = 2
W_PIECES = 4


def kernel(
    groups,
    experts,
    span,
    res_ref,
    gain_ref,
    router_ref,
    ids_ref,
    wg_in,
    wu_in,
    wd_in,
    out_ref,
    tok,
    gates,
    act,
    rx,
    wg,
    wu,
    wd,
    own_sem,
    tok_recv,
    tok_up,
    tok_dn,
    gate_recv,
    gate_up,
    gate_dn,
    ret_send,
    ret_recv,
    y_send,
    y_recv,
    x_send,
    x_recv,
    c_send,
    c_recv,
    cy_send,
    cy_recv,
    cx_send,
    cx_recv,
):
    rows, width = res_ref.shape
    hid = wg_in.shape[1]
    grp = lax.axis_index("groups")
    pos = lax.axis_index("expert")
    exp = pos // span
    mem = pos % span
    last = experts - 1
    has_up = exp < last
    has_dn = exp > 0
    base = exp * span
    mem_y = (mem + 2) % 4
    mem_c = mem + 1 - 2 * (mem % 2)
    mem_yc = (mem_c + 2) % 4
    up = {"groups": grp, "expert": jnp.minimum(pos + span, experts * span - 1)}
    dn = {"groups": grp, "expert": jnp.maximum(pos - span, 0)}
    to_y = {"groups": grp, "expert": base + mem_y}
    to_c = {"groups": grp, "expert": base + mem_c}

    def other(i):
        return (grp + 1 + i) % groups

    barrier = pltpu.get_barrier_semaphore()

    def greet(device):
        pl.semaphore_signal(barrier, inc=1, device_id=device, device_id_type=MESH)

    greet(to_y)
    greet(to_c)
    for i in range(groups - 1):
        greet({"groups": other(i), "expert": pos})

    @pl.when(has_up)
    def _():
        greet(up)

    @pl.when(has_dn)
    def _():
        greet(dn)

    peers = 1 + groups + has_up.astype(jnp.int32) + has_dn.astype(jnp.int32)
    pl.semaphore_wait(barrier, peers)

    mats = ((wg_in, wg), (wu_in, wu), (wd_in, wd))

    def piece(mat, group, index):
        total = mats[mat][0].shape[0]
        size = total // groups // W_PIECES
        return pl.ds(pl.multiple_of(group * (total // groups) + index * size, size), size)

    def remote(src, dst, send, recv, device):
        return pltpu.make_async_remote_copy(
            src_ref=src, dst_ref=dst, send_sem=send, recv_sem=recv, device_id=device, device_id_type=MESH
        )

    def y_copy(mat, index, landing):
        part = piece(mat, grp, index)
        at = mat * W_PIECES + index
        slot = mem_y if landing else mem
        return remote(mats[mat][0].at[part], mats[mat][1].at[slot, part], y_send.at[at], y_recv.at[at], to_y)

    def x_copy(mat, index, i, landing):
        at = mat * W_PIECES + index
        group = (grp + groups - 1 - i) % groups if landing else grp
        part = piece(mat, group, index)
        ref = mats[mat][1].at[mem_y, part]
        return remote(ref, ref, x_send.at[i, at], x_recv.at[i, at], {"groups": other(i), "expert": pos})

    def cy_copy(mat, index, landing):
        at = mat * W_PIECES + index
        part = piece(mat, grp, index)
        ref = mats[mat][1].at[mem_yc if landing else mem_y, part]
        return remote(ref, ref, cy_send.at[at], cy_recv.at[at], to_c)

    def cx_copy(mat, index, i, landing):
        at = mat * W_PIECES + index
        part = piece(mat, (grp + groups - 1 - i) % groups, index)
        ref = mats[mat][1].at[mem_yc if landing else mem_y, part]
        return remote(ref, ref, cx_send.at[i, at], cx_recv.at[i, at], to_c)

    def c_copy(mat, landing):
        slot = mem_c if landing else mem
        return remote(mats[mat][0], mats[mat][1].at[slot], c_send.at[mat], c_recv.at[mat], to_c)

    for mat in range(3):
        for index in range(W_PIECES):
            y_copy(mat, index, False).start()
    own_copies = [pltpu.make_async_copy(mats[i][0], mats[i][1].at[mem], own_sem.at[i]) for i in range(3)]
    for mat in range(3):
        c_copy(mat, False).start()
        own_copies[mat].start()

    step_rows = 16

    def norm_rows(i, carry):
        at = pl.ds(pl.multiple_of(i * step_rows, step_rows), step_rows)
        wide = res_ref[at, :].astype(jnp.float32)
        mean = jnp.mean(wide * wide, axis=1, keepdims=True)
        tok[exp, at, :] = (wide * lax.rsqrt(mean + norm_eps) * gain_ref[...]).astype(jnp.bfloat16)
        return carry

    lax.fori_loop(0, rows // step_rows, norm_rows, 0)
    piece_rows = rows // TOK_PIECES

    def tok_copy(block, index, upward):
        ref = tok.at[block, pl.ds(index * piece_rows, piece_rows)]
        send = (tok_up if upward else tok_dn).at[block, index]
        return remote(ref, ref, send, tok_recv.at[block, index], up if upward else dn)

    def gate_copy(block, upward):
        ref = gates.at[block]
        send = (gate_up if upward else gate_dn).at[block]
        return remote(ref, ref, send, gate_recv.at[block], up if upward else dn)

    def send_block(block, index, upward):
        tok_copy(block, index, upward).start()
        if index == 0:
            gate_copy(block, upward).start()

    def gate_values():
        logits = jnp.dot(tok[exp], router_ref[...], preferred_element_type=jnp.float32)
        affinity = jax.nn.sigmoid(logits)
        lane = lax.broadcasted_iota(jnp.int32, (rows, LANES), 1)
        total = jnp.zeros((rows, 1), jnp.float32)
        spread = jnp.zeros((rows, LANES), jnp.float32)
        for k in range(ids_ref.shape[1]):
            chosen = jnp.where(lane == ids_ref[:, k : k + 1], affinity, 0.0)
            total = total + jnp.sum(chosen, axis=1, keepdims=True)
            spread = spread + chosen
        values = route_scale * spread / total
        gates[exp] = values.T[: gates.shape[1]]

    gate_values()

    @pl.when(has_up)
    def _():
        for index in range(TOK_PIECES):
            send_block(exp, index, True)

    @pl.when(has_dn)
    def _():
        for index in range(TOK_PIECES):
            send_block(exp, index, False)

    def weight_tick(mat, index):
        y_copy(mat, index, True).wait_recv()
        for i in range(groups - 1):
            x_copy(mat, index, i, False).start()
        cy_copy(mat, index, False).start()

    def weight_late(mat, index):
        for i in range(groups - 1):
            x_copy(mat, index, i, True).wait_recv()
            cx_copy(mat, index, i, False).start()

    def token_tick(step, index):
        low = exp - step
        high = exp + step

        @pl.when(low >= 0)
        def _():
            tok_copy(jnp.maximum(low, 0), index, True).wait_recv()
            if index == 0:
                gate_copy(jnp.maximum(low, 0), True).wait_recv()

        @pl.when(jnp.logical_and(low >= 0, has_up))
        def _():
            send_block(jnp.maximum(low, 0), index, True)

        @pl.when(high <= last)
        def _():
            tok_copy(jnp.minimum(high, last), index, False).wait_recv()
            if index == 0:
                gate_copy(jnp.minimum(high, last), False).wait_recv()

        @pl.when(jnp.logical_and(high <= last, has_dn))
        def _():
            send_block(jnp.minimum(high, last), index, False)

    def hidden_part(block, slot):
        rows_in = tok[block]
        gate_proj = jnp.dot(rows_in, wg[slot], preferred_element_type=jnp.float32)
        up_proj = jnp.dot(rows_in, wu[slot], preferred_element_type=jnp.float32)
        sublane = lax.broadcasted_iota(jnp.int32, (gates.shape[1], rows), 0)
        row = jnp.sum(jnp.where(sublane == exp, gates[block], 0.0), axis=0, keepdims=True)
        scale = jnp.broadcast_to(row, (LANES, rows)).T[:, :1]
        hidden = gate_proj / (1.0 + jnp.exp(-gate_proj)) * up_proj * scale
        act[slot, block] = hidden.astype(jnp.bfloat16)

    def hidden_of(block, slots):
        def body(slot, carry):
            hidden_part(block, slot)
            return carry

        lax.fori_loop(0, slots, body, 0)

    def hidden_ready():
        for mat in range(2):
            own_copies[mat].wait()
            c_copy(mat, True).wait_recv()
            for index in range(W_PIECES):
                cy_copy(mat, index, True).wait_recv()
                for i in range(groups - 1):
                    cx_copy(mat, index, i, True).wait_recv()

    events = []
    weight_steps = 3 * W_PIECES
    for tick in range(weight_steps):
        mat, index = divmod(tick, W_PIECES)
        events.append(((tick + 1) / weight_steps, 0, functools.partial(weight_tick, mat, index)))
        events.append(((tick + 2) / weight_steps, 1, functools.partial(weight_late, mat, index)))
    token_steps = last * TOK_PIECES
    for tick in range(token_steps):
        step, index = divmod(tick, TOK_PIECES)
        events.append(((tick + 1) / token_steps, 2, functools.partial(token_tick, step + 1, index)))
    events.sort(key=lambda event: event[:2])
    for event in events:
        event[2]()
    hidden_ready()

    def hidden_body(block, carry):
        hidden_of(block, span)
        return carry

    lax.fori_loop(0, experts, hidden_body, 0)

    own_copies[2].wait()
    c_copy(2, True).wait_recv()
    for index in range(W_PIECES):
        cy_copy(2, index, True).wait_recv()
        for i in range(groups - 1):
            cx_copy(2, index, i, True).wait_recv()

    def sent(block, carry):
        @pl.when(jnp.logical_and(block <= exp, has_up))
        def _():
            for index in range(TOK_PIECES):
                tok_copy(block, index, True).wait_send()
            gate_copy(block, True).wait_send()

        @pl.when(jnp.logical_and(block >= exp, has_dn))
        def _():
            for index in range(TOK_PIECES):
                tok_copy(block, index, False).wait_send()
            gate_copy(block, False).wait_send()

        return carry

    lax.fori_loop(0, experts, sent, 0)

    cols = width // OUT_PIECES
    tile = 256

    def out_copy(block, index, upward, landing):
        part = pl.ds(index * cols, cols)
        into = block
        if not upward:
            target = exp if landing else exp - 1
            into = jnp.where(block == target, experts, block)
        return remote(
            tok.at[block, :, part],
            rx.at[into, :, part],
            ret_send.at[block, index],
            ret_recv.at[into, index],
            up if upward else dn,
        )

    def share(block, at):
        total = jnp.dot(act[0, block], wd[0, :, at], preferred_element_type=jnp.float32)
        for slot in range(1, span):
            total = total + jnp.dot(act[slot, block], wd[slot, :, at], preferred_element_type=jnp.float32)
        return total

    def send_result(block, upward):
        joins = (exp > 0) if upward else (exp < last)
        for index in range(OUT_PIECES):

            @pl.when(joins)
            def _():
                out_copy(block, index, upward, True).wait_recv()

                def body(i, carry):
                    at = pl.ds(pl.multiple_of(index * cols + i * tile, tile), tile)
                    total = share(block, at) + rx[block, :, at].astype(jnp.float32)
                    tok[block, :, at] = total.astype(jnp.bfloat16)
                    return carry

                lax.fori_loop(0, cols // tile, body, 0)

            @pl.when(jnp.logical_not(joins))
            def _():
                def body(i, carry):
                    at = pl.ds(pl.multiple_of(index * cols + i * tile, tile), tile)
                    tok[block, :, at] = share(block, at).astype(jnp.bfloat16)
                    return carry

                lax.fori_loop(0, cols // tile, body, 0)

            out_copy(block, index, upward, False).start()

    def return_step(step, carry):
        low = exp - (experts - step)
        high = exp + (experts - step)

        @pl.when(low >= 0)
        def _():
            send_result(jnp.maximum(low, 0), False)

        @pl.when(high <= last)
        def _():
            send_result(jnp.minimum(high, last), True)

        return carry

    lax.fori_loop(1, experts, return_step, 0)

    def finish(index):
        @pl.when(has_dn)
        def _():
            out_copy(exp, index, True, True).wait_recv()

        @pl.when(has_up)
        def _():
            out_copy(exp, index, False, True).wait_recv()

        def body(i, carry):
            at = pl.ds(pl.multiple_of(index * cols + i * tile, tile), tile)
            total = res_ref[:, at].astype(jnp.float32) + share(exp, at)
            below = jnp.where(has_dn, rx[exp, :, at].astype(jnp.float32), 0.0)
            above = jnp.where(has_up, rx[experts, :, at].astype(jnp.float32), 0.0)
            out_ref[:, at] = (total + below + above).astype(jnp.bfloat16)
            return carry

        lax.fori_loop(0, cols // tile, body, 0)

    for index in range(OUT_PIECES):
        finish(index)

    def results_sent(block, carry):
        @pl.when(block < exp)
        def _():
            for index in range(OUT_PIECES):
                out_copy(block, index, False, False).wait_send()

        @pl.when(block > exp)
        def _():
            for index in range(OUT_PIECES):
                out_copy(block, index, True, False).wait_send()

        return carry

    lax.fori_loop(0, experts, results_sent, 0)
    for mat in range(3):
        c_copy(mat, False).wait_send()
        for index in range(W_PIECES):
            y_copy(mat, index, False).wait_send()
            cy_copy(mat, index, False).wait_send()
            for i in range(groups - 1):
                x_copy(mat, index, i, False).wait_send()
                cx_copy(mat, index, i, False).wait_send()


def shards(residual, norm_gain, router, w_gate, w_up, w_down, expert_ids):
    rows, width = residual.shape
    experts = router.shape[1]
    groups = lax.axis_size("groups")
    span = lax.axis_size("expert") // experts
    assert span == 4
    hid = w_gate.shape[1]
    gate_rows = max(8, experts)
    wide_router = jnp.pad(router, ((0, 0), (0, LANES - experts)))
    vmem = pl.BlockSpec(memory_space=pltpu.VMEM)
    anywhere = pl.BlockSpec(memory_space=pl.ANY)
    dma = pltpu.SemaphoreType.DMA
    weight_copies = 3 * W_PIECES
    return pl.pallas_call(
        functools.partial(kernel, groups, experts, span),
        out_shape=jax.ShapeDtypeStruct((rows, width), jnp.bfloat16),
        in_specs=[vmem, vmem, vmem, vmem, anywhere, anywhere, anywhere],
        out_specs=vmem,
        scratch_shapes=[
            pltpu.VMEM((experts, rows, width), jnp.bfloat16),
            pltpu.VMEM((experts, gate_rows, rows), jnp.float32),
            pltpu.VMEM((span, experts, rows, hid), jnp.bfloat16),
            pltpu.VMEM((experts + 1, rows, width), jnp.bfloat16),
            pltpu.VMEM((span, width, hid), jnp.bfloat16),
            pltpu.VMEM((span, width, hid), jnp.bfloat16),
            pltpu.VMEM((span, hid, width), jnp.bfloat16),
            dma((3,)),
            dma((experts, TOK_PIECES)),
            dma((experts, TOK_PIECES)),
            dma((experts, TOK_PIECES)),
            dma((experts,)),
            dma((experts,)),
            dma((experts,)),
            dma((experts, OUT_PIECES)),
            dma((experts + 1, OUT_PIECES)),
            dma((weight_copies,)),
            dma((weight_copies,)),
            dma((groups - 1, weight_copies)),
            dma((groups - 1, weight_copies)),
            dma((3,)),
            dma((3,)),
            dma((weight_copies,)),
            dma((weight_copies,)),
            dma((groups - 1, weight_copies)),
            dma((groups - 1, weight_copies)),
        ],
        compiler_params=pltpu.CompilerParams(
            collective_id=0, has_side_effects=True, vmem_limit_bytes=67043328
        ),
    )(residual, norm_gain.reshape(1, width), wide_router, expert_ids, w_gate, w_up, w_down)


def solution(mesh):
    in_specs = (
        P(("groups", "expert"), None),
        P(),
        P(),
        P(None, "expert"),
        P(None, "expert"),
        P("expert", None),
        P(("groups", "expert"), None),
    )
    out_specs = P(("groups", "expert"), None)
    return jax.shard_map(shards, mesh=mesh, in_specs=in_specs, out_specs=out_specs, check_vma=False)
```

```python
import functools

import jax
import jax.numpy as jnp
from jax import lax
from jax.experimental import pallas as pl
from jax.experimental.pallas import tpu as pltpu
from jax.sharding import PartitionSpec as P

route_scale = 2.5
norm_eps = 1e-06
LANES = 128
MESH = pl.DeviceIdType.MESH

TOK_PIECES = 2
OUT_PIECES = 2
W_PIECES = 4


def kernel(
    groups,
    experts,
    span,
    capacity,
    res_ref,
    gain_ref,
    router_ref,
    ids_ref,
    wg_in,
    wu_in,
    wd_in,
    out_ref,
    tok,
    gates,
    act,
    rx,
    acc,
    wg,
    wu,
    wd,
    own_sem,
    tok_recv,
    tok_up,
    tok_dn,
    gate_recv,
    gate_up,
    gate_dn,
    ret_send,
    ret_recv,
    y_send,
    y_recv,
    x_send,
    x_recv,
    c_send,
    c_recv,
    cy_send,
    cy_recv,
    cx_send,
    cx_recv,
):
    rows, width = res_ref.shape
    hid = wg_in.shape[1]
    grp = lax.axis_index("groups")
    pos = lax.axis_index("expert")
    exp = pos // span
    mem = pos % span
    last = experts - 1
    has_up = exp < last
    has_dn = exp > 0
    base = exp * span
    mem_y = (mem + 2) % 4
    mem_c = mem + 1 - 2 * (mem % 2)
    mem_yc = (mem_c + 2) % 4
    up = {"groups": grp, "expert": jnp.minimum(pos + span, experts * span - 1)}
    dn = {"groups": grp, "expert": jnp.maximum(pos - span, 0)}
    to_y = {"groups": grp, "expert": base + mem_y}
    to_c = {"groups": grp, "expert": base + mem_c}

    def other(i):
        return (grp + 1 + i) % groups

    barrier = pltpu.get_barrier_semaphore()

    def greet(device):
        pl.semaphore_signal(barrier, inc=1, device_id=device, device_id_type=MESH)

    greet(to_y)
    greet(to_c)
    for i in range(groups - 1):
        greet({"groups": other(i), "expert": pos})

    @pl.when(has_up)
    def _():
        greet(up)

    @pl.when(has_dn)
    def _():
        greet(dn)

    peers = 1 + groups + has_up.astype(jnp.int32) + has_dn.astype(jnp.int32)
    pl.semaphore_wait(barrier, peers)

    mats = ((wg_in, wg), (wu_in, wu), (wd_in, wd))

    def piece(mat, group, index):
        total = mats[mat][0].shape[0]
        size = total // groups // W_PIECES
        return pl.ds(pl.multiple_of(group * (total // groups) + index * size, size), size)

    def remote(src, dst, send, recv, device):
        return pltpu.make_async_remote_copy(
            src_ref=src, dst_ref=dst, send_sem=send, recv_sem=recv, device_id=device, device_id_type=MESH
        )

    def y_copy(mat, index, landing):
        part = piece(mat, grp, index)
        at = mat * W_PIECES + index
        slot = mem_y if landing else mem
        return remote(mats[mat][0].at[part], mats[mat][1].at[slot, part], y_send.at[at], y_recv.at[at], to_y)

    def x_copy(mat, index, i, landing):
        at = mat * W_PIECES + index
        group = (grp + groups - 1 - i) % groups if landing else grp
        part = piece(mat, group, index)
        ref = mats[mat][1].at[mem_y, part]
        return remote(ref, ref, x_send.at[i, at], x_recv.at[i, at], {"groups": other(i), "expert": pos})

    def cy_copy(mat, index, landing):
        at = mat * W_PIECES + index
        part = piece(mat, grp, index)
        ref = mats[mat][1].at[mem_yc if landing else mem_y, part]
        return remote(ref, ref, cy_send.at[at], cy_recv.at[at], to_c)

    def cx_copy(mat, index, i, landing):
        at = mat * W_PIECES + index
        part = piece(mat, (grp + groups - 1 - i) % groups, index)
        ref = mats[mat][1].at[mem_yc if landing else mem_y, part]
        return remote(ref, ref, cx_send.at[i, at], cx_recv.at[i, at], to_c)

    def c_copy(mat, landing):
        slot = mem_c if landing else mem
        return remote(mats[mat][0], mats[mat][1].at[slot], c_send.at[mat], c_recv.at[mat], to_c)

    for mat in range(3):
        for index in range(W_PIECES):
            y_copy(mat, index, False).start()
    own_copies = [pltpu.make_async_copy(mats[i][0], mats[i][1].at[mem], own_sem.at[i]) for i in range(3)]
    for mat in range(3):
        c_copy(mat, False).start()
        own_copies[mat].start()

    step_rows = 16

    def norm_rows(i, carry):
        at = pl.ds(pl.multiple_of(i * step_rows, step_rows), step_rows)
        wide = res_ref[at, :].astype(jnp.float32)
        mean = jnp.mean(wide * wide, axis=1, keepdims=True)
        tok[exp, at, :] = (wide * lax.rsqrt(mean + norm_eps) * gain_ref[...].reshape(1, width)).astype(jnp.bfloat16)
        return carry

    lax.fori_loop(0, rows // step_rows, norm_rows, 0)
    piece_rows = rows // TOK_PIECES

    def tok_copy(block, index, upward):
        ref = tok.at[block, pl.ds(index * piece_rows, piece_rows)]
        send = (tok_up if upward else tok_dn).at[block, index]
        return remote(ref, ref, send, tok_recv.at[block, index], up if upward else dn)

    def gate_copy(block, upward):
        ref = gates.at[block]
        send = (gate_up if upward else gate_dn).at[block]
        return remote(ref, ref, send, gate_recv.at[block], up if upward else dn)

    def send_block(block, index, upward):
        tok_copy(block, index, upward).start()
        if index == 0:
            gate_copy(block, upward).start()

    def gate_values():
        logits = lax.dot_general(
            router_ref[...], tok[exp], (((1,), (1,)), ((), ())), preferred_element_type=jnp.float32
        )
        affinity = jax.nn.sigmoid(logits)
        expert = lax.broadcasted_iota(jnp.int32, (experts, rows), 0)
        spread = jnp.zeros((experts, rows), jnp.float32)
        for k in range(ids_ref.shape[0]):
            spread = spread + jnp.where(expert == ids_ref[k : k + 1, :], affinity, 0.0)
        gates[exp] = route_scale * spread / jnp.sum(spread, axis=0, keepdims=True)

    gate_values()

    @pl.when(has_up)
    def _():
        for index in range(TOK_PIECES):
            send_block(exp, index, True)

    @pl.when(has_dn)
    def _():
        for index in range(TOK_PIECES):
            send_block(exp, index, False)

    def weight_tick(mat, index):
        y_copy(mat, index, True).wait_recv()
        for i in range(groups - 1):
            x_copy(mat, index, i, False).start()
        cy_copy(mat, index, False).start()

    def weight_late(mat, index):
        for i in range(groups - 1):
            x_copy(mat, index, i, True).wait_recv()
            cx_copy(mat, index, i, False).start()

    def token_tick(step, index):
        low = exp - step
        high = exp + step

        @pl.when(low >= 0)
        def _():
            tok_copy(jnp.maximum(low, 0), index, True).wait_recv()
            if index == 0:
                gate_copy(jnp.maximum(low, 0), True).wait_recv()

        @pl.when(jnp.logical_and(low >= 0, has_up))
        def _():
            send_block(jnp.maximum(low, 0), index, True)

        @pl.when(high <= last)
        def _():
            tok_copy(jnp.minimum(high, last), index, False).wait_recv()
            if index == 0:
                gate_copy(jnp.minimum(high, last), False).wait_recv()

        @pl.when(jnp.logical_and(high <= last, has_dn))
        def _():
            send_block(jnp.minimum(high, last), index, False)

    def hidden_part(block, slot):
        rows_in = tok[block]
        gate_proj = jnp.dot(rows_in, wg[slot], preferred_element_type=jnp.float32)
        up_proj = jnp.dot(rows_in, wu[slot], preferred_element_type=jnp.float32)
        sublane = lax.broadcasted_iota(jnp.int32, (gates.shape[1], rows), 0)
        row = jnp.sum(jnp.where(sublane == exp, gates[block], 0.0), axis=0, keepdims=True)
        scale = jnp.broadcast_to(row, (LANES, rows)).T[:, :1]
        hidden = gate_proj / (1.0 + jnp.exp(-gate_proj)) * up_proj * scale
        act[slot, block] = hidden.astype(jnp.bfloat16)

    def first_slices():
        for mat in range(2):
            own_copies[mat].wait()
            c_copy(mat, True).wait_recv()

    def all_slices():
        for mat in range(2):
            for index in range(W_PIECES):
                cy_copy(mat, index, True).wait_recv()
                for i in range(groups - 1):
                    cx_copy(mat, index, i, True).wait_recv()

    def hidden_step(step, first, second, count=2):
        def body(i, carry):
            side = i // count
            turn = i % count
            block = exp - step + 2 * step * side
            slot = jnp.where(turn == 0, first, jnp.where(turn == 1, second, jnp.where(turn == 2, mem_y, mem_yc)))

            @pl.when(jnp.logical_and(block >= 0, block <= last))
            def _():
                hidden_part(jnp.clip(block, 0, last), slot)

            return carry

        lax.fori_loop(0, count if step == 0 else 2 * count, body, 0)

    events = []
    weight_steps = 3 * W_PIECES
    for tick in range(weight_steps):
        mat, index = divmod(tick, W_PIECES)
        events.append(((tick + 1) / weight_steps, 0, functools.partial(weight_tick, mat, index)))
        events.append(((tick + 2) / weight_steps, 1, functools.partial(weight_late, mat, index)))
    token_steps = last * TOK_PIECES
    for tick in range(token_steps):
        step, index = divmod(tick, TOK_PIECES)
        events.append(((tick + 1) / token_steps, 2, functools.partial(token_tick, step + 1, index)))
    ready = (2 * W_PIECES + 2) / weight_steps
    events.append((1.5 / weight_steps, 3, first_slices))
    events.append((ready, 3, all_slices))
    for step in range(experts):
        there = max(step / last, 1.5 / weight_steps)
        if there >= ready:
            events.append((there, 4, functools.partial(hidden_step, step, mem, mem_c, span)))
        else:
            events.append((there, 4, functools.partial(hidden_step, step, mem, mem_c)))
            late = ready + 0.4 * step / weight_steps
            events.append((late, 4, functools.partial(hidden_step, step, mem_y, mem_yc)))
    events.sort(key=lambda event: event[:2])
    for event in events:
        event[2]()

    own_copies[2].wait()
    c_copy(2, True).wait_recv()
    for index in range(W_PIECES):
        cy_copy(2, index, True).wait_recv()
        for i in range(groups - 1):
            cx_copy(2, index, i, True).wait_recv()

    def sent(block, carry):
        @pl.when(jnp.logical_and(block <= exp, has_up))
        def _():
            for index in range(TOK_PIECES):
                tok_copy(block, index, True).wait_send()
            gate_copy(block, True).wait_send()

        @pl.when(jnp.logical_and(block >= exp, has_dn))
        def _():
            for index in range(TOK_PIECES):
                tok_copy(block, index, False).wait_send()
            gate_copy(block, False).wait_send()

        return carry

    lax.fori_loop(0, experts, sent, 0)

    cols = width // OUT_PIECES
    tile = 256

    def out_copy(block, index, upward, landing, packed):
        part = pl.ds(index * cols, cols)
        height = pl.ds(0, capacity if packed else rows)
        into = block
        if not upward:
            target = exp if landing else exp - 1
            into = jnp.where(block == target, experts, block)
        return remote(
            tok.at[block, height, part],
            rx.at[into, height, part],
            ret_send.at[block, index],
            ret_recv.at[into, index],
            up if upward else dn,
        )

    def share(block, at, height=rows):
        part = pl.ds(0, height)
        total = jnp.dot(act[0, block, part], wd[0, :, at], preferred_element_type=jnp.float32)
        for slot in range(1, span):
            total = total + jnp.dot(act[slot, block, part], wd[slot, :, at], preferred_element_type=jnp.float32)
        return total

    def packing(block, expert):
        sublane = lax.broadcasted_iota(jnp.int32, (gates.shape[1], rows), 0)
        row = jnp.sum(jnp.where(sublane == expert, gates[block], 0.0), axis=0, keepdims=True)
        taken = jnp.broadcast_to(jnp.where(row != 0.0, 1.0, 0.0), (capacity, rows))
        source = lax.broadcasted_iota(jnp.int32, (rows, rows), 0)
        dest = lax.broadcasted_iota(jnp.int32, (rows, rows), 1)
        earlier = jnp.where(source < dest, 1.0, 0.0).astype(jnp.bfloat16)
        rank = jnp.dot(taken.astype(jnp.bfloat16), earlier, preferred_element_type=jnp.float32)
        slot = lax.broadcasted_iota(jnp.int32, (capacity, rows), 0).astype(jnp.float32)
        return jnp.where(rank == slot, taken, 0.0).astype(jnp.bfloat16)

    def unpacked(picks, value):
        return lax.dot_general(picks, value, (((0,), (0,)), ((), ())), preferred_element_type=jnp.float32)

    def tiles_of(index, body):
        def run(i, carry):
            body(pl.ds(pl.multiple_of(index * cols + i * tile, tile), tile))
            return carry

        lax.fori_loop(0, cols // tile, run, 0)

    def neighbour(upward):
        return exp - 1 if upward else exp + 1

    def is_end(expert, upward):
        return expert == (0 if upward else last)

    def send_result(block, index, upward):
        first = is_end(exp, upward)
        second = is_end(neighbour(upward), upward)

        @pl.when(first)
        def _():
            if index == 0:
                picks = packing(block, exp)
                for slot in range(span):
                    act[slot, block, pl.ds(0, capacity)] = jnp.dot(
                        picks, act[slot, block], preferred_element_type=jnp.float32
                    ).astype(jnp.bfloat16)

            def body(at):
                tok[block, pl.ds(0, capacity), at] = share(block, at, capacity).astype(jnp.bfloat16)

            tiles_of(index, body)
            out_copy(block, index, upward, False, True).start()

        @pl.when(second)
        def _():
            out_copy(block, index, upward, True, True).wait_recv()
            picks = packing(block, neighbour(upward))

            def body(at):
                total = share(block, at) + unpacked(picks, rx[block, pl.ds(0, capacity), at])
                tok[block, :, at] = total.astype(jnp.bfloat16)

            tiles_of(index, body)

        @pl.when(jnp.logical_not(jnp.logical_or(first, second)))
        def _():
            out_copy(block, index, upward, True, False).wait_recv()

            def body(at):
                total = share(block, at) + rx[block, :, at].astype(jnp.float32)
                tok[block, :, at] = total.astype(jnp.bfloat16)

            tiles_of(index, body)

        @pl.when(jnp.logical_not(first))
        def _():
            out_copy(block, index, upward, False, False).start()

    def return_step(step, carry):
        low = exp - (experts - step)
        high = exp + (experts - step)
        for index in range(OUT_PIECES):

            @pl.when(low >= 0)
            def _():
                send_result(jnp.maximum(low, 0), index, False)

            @pl.when(high <= last)
            def _():
                send_result(jnp.minimum(high, last), index, True)

        return carry

    lax.fori_loop(1, experts, return_step, 0)

    def own_body(i, carry):
        at = pl.ds(pl.multiple_of(i * tile, tile), tile)
        acc[:, at] = res_ref[:, at].astype(jnp.float32) + share(exp, at)
        return carry

    lax.fori_loop(0, width // tile, own_body, 0)

    def join(index, upward):
        slot = exp if upward else experts
        second = is_end(neighbour(upward), upward)

        @pl.when(second)
        def _():
            out_copy(exp, index, upward, True, True).wait_recv()
            picks = packing(exp, neighbour(upward))

            def body(at):
                acc[:, at] += unpacked(picks, rx[slot, pl.ds(0, capacity), at])

            tiles_of(index, body)

        @pl.when(jnp.logical_not(jnp.logical_or(second, is_end(exp, upward))))
        def _():
            out_copy(exp, index, upward, True, False).wait_recv()

            def body(at):
                acc[:, at] += rx[slot, :, at].astype(jnp.float32)

            tiles_of(index, body)

    for index in range(OUT_PIECES):
        join(index, True)
        join(index, False)

        def write(at):
            out_ref[:, at] = acc[:, at].astype(jnp.bfloat16)

        tiles_of(index, write)

    def wait_result(block, upward):
        first = is_end(exp, upward)

        @pl.when(first)
        def _():
            for index in range(OUT_PIECES):
                out_copy(block, index, upward, False, True).wait_send()

        @pl.when(jnp.logical_not(first))
        def _():
            for index in range(OUT_PIECES):
                out_copy(block, index, upward, False, False).wait_send()

    def results_sent(block, carry):
        @pl.when(block < exp)
        def _():
            wait_result(block, False)

        @pl.when(block > exp)
        def _():
            wait_result(block, True)

        return carry

    lax.fori_loop(0, experts, results_sent, 0)
    for mat in range(3):
        c_copy(mat, False).wait_send()
        for index in range(W_PIECES):
            y_copy(mat, index, False).wait_send()
            cy_copy(mat, index, False).wait_send()
            for i in range(groups - 1):
                x_copy(mat, index, i, False).wait_send()
                cx_copy(mat, index, i, False).wait_send()


def shards(residual, norm_gain, router, w_gate, w_up, w_down, expert_ids):
    rows, width = residual.shape
    experts = router.shape[1]
    groups = lax.axis_size("groups")
    span = lax.axis_size("expert") // experts
    assert span == 4
    hid = w_gate.shape[1]
    capacity = 3 * rows * expert_ids.shape[1] // (2 * experts)
    capacity = min(rows, -(-capacity // 16) * 16)
    vmem = pl.BlockSpec(memory_space=pltpu.VMEM)
    anywhere = pl.BlockSpec(memory_space=pl.ANY)
    dma = pltpu.SemaphoreType.DMA
    weight_copies = 3 * W_PIECES
    return pl.pallas_call(
        functools.partial(kernel, groups, experts, span, capacity),
        out_shape=jax.ShapeDtypeStruct((rows, width), jnp.bfloat16),
        in_specs=[vmem, vmem, vmem, vmem, anywhere, anywhere, anywhere],
        out_specs=vmem,
        scratch_shapes=[
            pltpu.VMEM((experts, rows, width), jnp.bfloat16),
            pltpu.VMEM((experts, experts, rows), jnp.float32),
            pltpu.VMEM((span, experts, rows, hid), jnp.bfloat16),
            pltpu.VMEM((experts + 1, rows, width), jnp.bfloat16),
            pltpu.VMEM((rows, width), jnp.float32),
            pltpu.VMEM((span, width, hid), jnp.bfloat16),
            pltpu.VMEM((span, width, hid), jnp.bfloat16),
            pltpu.VMEM((span, hid, width), jnp.bfloat16),
            dma((3,)),
            dma((experts, TOK_PIECES)),
            dma((experts, TOK_PIECES)),
            dma((experts, TOK_PIECES)),
            dma((experts,)),
            dma((experts,)),
            dma((experts,)),
            dma((experts, OUT_PIECES)),
            dma((experts + 1, OUT_PIECES)),
            dma((weight_copies,)),
            dma((weight_copies,)),
            dma((groups - 1, weight_copies)),
            dma((groups - 1, weight_copies)),
            dma((3,)),
            dma((3,)),
            dma((weight_copies,)),
            dma((weight_copies,)),
            dma((groups - 1, weight_copies)),
            dma((groups - 1, weight_copies)),
        ],
        compiler_params=pltpu.CompilerParams(
            collective_id=0, has_side_effects=True, vmem_limit_bytes=67043328
        ),
    )(residual, norm_gain, router.T, expert_ids.T, w_gate, w_up, w_down)


def solution(mesh):
    in_specs = (
        P(("groups", "expert"), None),
        P(),
        P(),
        P(None, "expert"),
        P(None, "expert"),
        P("expert", None),
        P(("groups", "expert"), None),
    )
    out_specs = P(("groups", "expert"), None)
    return jax.shard_map(shards, mesh=mesh, in_specs=in_specs, out_specs=out_specs, check_vma=False)
```

```python
import functools

import jax
import jax.numpy as jnp
from jax import lax
from jax.experimental import pallas as pl
from jax.experimental.pallas import tpu as pltpu
from jax.sharding import PartitionSpec as P

route_scale = 2.5
norm_eps = 1e-06
LANES = 128
MESH = pl.DeviceIdType.MESH

TOK_PIECES = 2
OUT_PIECES = 7
W_PIECES = (4, 4, 7)


def kernel(
    groups,
    experts,
    span,
    capacity,
    res_ref,
    gain_ref,
    router_ref,
    ids_ref,
    wg_in,
    wu_in,
    wd_in,
    out_ref,
    tok,
    gates,
    act,
    rx,
    acc,
    wg,
    wu,
    wd,
    own_sem,
    tok_recv,
    tok_up,
    tok_dn,
    gate_recv,
    gate_up,
    gate_dn,
    ret_send,
    ret_recv,
    y_send,
    y_recv,
    x_send,
    x_recv,
    c_send,
    c_recv,
    cy_send,
    cy_recv,
    cx_send,
    cx_recv,
):
    rows, width = res_ref.shape
    hid = wg_in.shape[1]
    grp = lax.axis_index("groups")
    pos = lax.axis_index("expert")
    exp = pos // span
    mem = pos % span
    last = experts - 1
    has_up = exp < last
    has_dn = exp > 0
    base = exp * span
    mem_y = (mem + 2) % 4
    mem_c = mem + 1 - 2 * (mem % 2)
    mem_yc = (mem_c + 2) % 4
    up = {"groups": grp, "expert": jnp.minimum(pos + span, experts * span - 1)}
    dn = {"groups": grp, "expert": jnp.maximum(pos - span, 0)}
    to_y = {"groups": grp, "expert": base + mem_y}
    to_c = {"groups": grp, "expert": base + mem_c}

    def other(i):
        return (grp + 1 + i) % groups

    barrier = pltpu.get_barrier_semaphore()

    def greet(device):
        pl.semaphore_signal(barrier, inc=1, device_id=device, device_id_type=MESH)

    greet(to_y)
    greet(to_c)
    for i in range(groups - 1):
        greet({"groups": other(i), "expert": pos})

    @pl.when(has_up)
    def _():
        greet(up)

    @pl.when(has_dn)
    def _():
        greet(dn)

    peers = 1 + groups + has_up.astype(jnp.int32) + has_dn.astype(jnp.int32)
    pl.semaphore_wait(barrier, peers)

    mats = ((wg_in, wg), (wu_in, wu), (wd_in, wd))

    def piece(ref, mat, group, index):
        total = mats[mat][0].shape[mat // 2]
        size = total // groups // W_PIECES[mat]
        part = pl.ds(pl.multiple_of(group * (total // groups) + index * size, size), size)
        return ref.at[:, part] if mat == 2 else ref.at[part]

    def number(mat, index):
        return sum(W_PIECES[:mat]) + index

    def remote(src, dst, send, recv, device):
        return pltpu.make_async_remote_copy(
            src_ref=src, dst_ref=dst, send_sem=send, recv_sem=recv, device_id=device, device_id_type=MESH
        )

    def y_copy(mat, index, landing):
        at = number(mat, index)
        into = piece(mats[mat][1].at[mem_y if landing else mem], mat, grp, index)
        return remote(piece(mats[mat][0], mat, grp, index), into, y_send.at[at], y_recv.at[at], to_y)

    def x_copy(mat, index, i, landing):
        at = number(mat, index)
        group = (grp + groups - 1 - i) % groups if landing else grp
        ref = piece(mats[mat][1].at[mem_y], mat, group, index)
        return remote(ref, ref, x_send.at[i, at], x_recv.at[i, at], {"groups": other(i), "expert": pos})

    def cy_copy(mat, index, landing):
        at = number(mat, index)
        ref = piece(mats[mat][1].at[mem_yc if landing else mem_y], mat, grp, index)
        return remote(ref, ref, cy_send.at[at], cy_recv.at[at], to_c)

    def cx_copy(mat, index, i, landing):
        at = number(mat, index)
        group = (grp + groups - 1 - i) % groups
        ref = piece(mats[mat][1].at[mem_yc if landing else mem_y], mat, group, index)
        return remote(ref, ref, cx_send.at[i, at], cx_recv.at[i, at], to_c)

    def c_copy(mat, landing):
        slot = mem_c if landing else mem
        return remote(mats[mat][0], mats[mat][1].at[slot], c_send.at[mat], c_recv.at[mat], to_c)

    for mat in range(3):
        for index in range(W_PIECES[mat]):
            y_copy(mat, index, False).start()
    own_copies = [pltpu.make_async_copy(mats[i][0], mats[i][1].at[mem], own_sem.at[i]) for i in range(3)]
    for mat in range(3):
        c_copy(mat, False).start()
        own_copies[mat].start()

    step_rows = 16

    def norm_rows(i, carry):
        at = pl.ds(pl.multiple_of(i * step_rows, step_rows), step_rows)
        wide = res_ref[at, :].astype(jnp.float32)
        mean = jnp.mean(wide * wide, axis=1, keepdims=True)
        tok[exp, at, :] = (wide * lax.rsqrt(mean + norm_eps) * gain_ref[...].reshape(1, width)).astype(jnp.bfloat16)
        return carry

    piece_rows = rows // TOK_PIECES

    def tok_copy(block, index, upward):
        ref = tok.at[block, pl.ds(index * piece_rows, piece_rows)]
        send = (tok_up if upward else tok_dn).at[block, index]
        return remote(ref, ref, send, tok_recv.at[block, index], up if upward else dn)

    def gate_copy(block, upward):
        ref = gates.at[block]
        send = (gate_up if upward else gate_dn).at[block]
        return remote(ref, ref, send, gate_recv.at[block], up if upward else dn)

    def send_block(block, index, upward):
        tok_copy(block, index, upward).start()
        if index == TOK_PIECES - 1:
            gate_copy(block, upward).start()

    def gate_values():
        logits = lax.dot_general(
            router_ref[...], tok[exp], (((1,), (1,)), ((), ())), preferred_element_type=jnp.float32
        )
        affinity = jax.nn.sigmoid(logits)
        expert = lax.broadcasted_iota(jnp.int32, (experts, rows), 0)
        spread = jnp.zeros((experts, rows), jnp.float32)
        for k in range(ids_ref.shape[0]):
            spread = spread + jnp.where(expert == ids_ref[k : k + 1, :], affinity, 0.0)
        gates[exp] = route_scale * spread / jnp.sum(spread, axis=0, keepdims=True)

    steps = piece_rows // step_rows
    for index in range(TOK_PIECES):
        lax.fori_loop(index * steps, (index + 1) * steps, norm_rows, 0)

        @pl.when(has_up)
        def _():
            tok_copy(exp, index, True).start()

        @pl.when(has_dn)
        def _():
            tok_copy(exp, index, False).start()

    gate_values()

    @pl.when(has_up)
    def _():
        gate_copy(exp, True).start()

    @pl.when(has_dn)
    def _():
        gate_copy(exp, False).start()

    def weight_tick(mat, index):
        y_copy(mat, index, True).wait_recv()
        for i in range(groups - 1):
            x_copy(mat, index, i, False).start()
        cy_copy(mat, index, False).start()

    def weight_late(mat, index):
        for i in range(groups - 1):
            x_copy(mat, index, i, True).wait_recv()
            cx_copy(mat, index, i, False).start()

    def token_tick(step, index):
        low = exp - step
        high = exp + step

        @pl.when(low >= 0)
        def _():
            tok_copy(jnp.maximum(low, 0), index, True).wait_recv()
            if index == TOK_PIECES - 1:
                gate_copy(jnp.maximum(low, 0), True).wait_recv()

        @pl.when(jnp.logical_and(low >= 0, has_up))
        def _():
            send_block(jnp.maximum(low, 0), index, True)

        @pl.when(high <= last)
        def _():
            tok_copy(jnp.minimum(high, last), index, False).wait_recv()
            if index == TOK_PIECES - 1:
                gate_copy(jnp.minimum(high, last), False).wait_recv()

        @pl.when(jnp.logical_and(high <= last, has_dn))
        def _():
            send_block(jnp.minimum(high, last), index, False)

    def hidden_part(block, slot):
        rows_in = tok[block]
        gate_proj = jnp.dot(rows_in, wg[slot], preferred_element_type=jnp.float32)
        up_proj = jnp.dot(rows_in, wu[slot], preferred_element_type=jnp.float32)
        sublane = lax.broadcasted_iota(jnp.int32, (gates.shape[1], rows), 0)
        row = jnp.sum(jnp.where(sublane == exp, gates[block], 0.0), axis=0, keepdims=True)
        scale = jnp.broadcast_to(row, (LANES, rows)).T[:, :1]
        hidden = gate_proj / (1.0 + jnp.exp(-gate_proj)) * up_proj * scale
        act[slot, block] = hidden.astype(jnp.bfloat16)

    def first_slices():
        for mat in range(2):
            own_copies[mat].wait()
            c_copy(mat, True).wait_recv()

    def all_slices():
        for mat in range(2):
            for index in range(W_PIECES[mat]):
                cy_copy(mat, index, True).wait_recv()
                for i in range(groups - 1):
                    cx_copy(mat, index, i, True).wait_recv()

    def hidden_step(step, first, second, count=2):
        def body(i, carry):
            side = i // count
            turn = i % count
            block = exp - step + 2 * step * side
            slot = jnp.where(turn == 0, first, jnp.where(turn == 1, second, jnp.where(turn == 2, mem_y, mem_yc)))

            @pl.when(jnp.logical_and(block >= 0, block <= last))
            def _():
                hidden_part(jnp.clip(block, 0, last), slot)

            return carry

        lax.fori_loop(0, count if step == 0 else 2 * count, body, 0)

    events = []
    for mat in range(3):
        for index in range(W_PIECES[mat]):
            size = 1 / 3 / W_PIECES[mat]
            when = mat / 3 + (index + 1) * size
            events.append((when, 0, functools.partial(weight_tick, mat, index)))
            events.append((when + size, 1, functools.partial(weight_late, mat, index)))
    token_steps = last * TOK_PIECES
    for tick in range(token_steps):
        step, index = divmod(tick, TOK_PIECES)
        events.append(((tick + 1) / token_steps, 2, functools.partial(token_tick, step + 1, index)))
    ready = 0.83
    events.append((0.12, 3, first_slices))
    events.append((ready, 3, all_slices))
    for step in range(experts):
        there = max(step / last, 0.12)
        if there >= ready:
            events.append((there, 4, functools.partial(hidden_step, step, mem, mem_c, span)))
        else:
            events.append((there, 4, functools.partial(hidden_step, step, mem, mem_c)))
            late = ready + 0.04 * step
            events.append((late, 4, functools.partial(hidden_step, step, mem_y, mem_yc)))
    events.sort(key=lambda event: event[:2])
    for event in events:
        event[2]()

    own_copies[2].wait()
    c_copy(2, True).wait_recv()
    for index in range(W_PIECES[2]):
        cy_copy(2, index, True).wait_recv()
        for i in range(groups - 1):
            cx_copy(2, index, i, True).wait_recv()

    def sent(block, carry):
        @pl.when(jnp.logical_and(block <= exp, has_up))
        def _():
            for index in range(TOK_PIECES):
                tok_copy(block, index, True).wait_send()
            gate_copy(block, True).wait_send()

        @pl.when(jnp.logical_and(block >= exp, has_dn))
        def _():
            for index in range(TOK_PIECES):
                tok_copy(block, index, False).wait_send()
            gate_copy(block, False).wait_send()

        return carry

    lax.fori_loop(0, experts, sent, 0)

    cols = width // OUT_PIECES
    tile = 256

    def out_copy(block, index, upward, landing, packed):
        part = pl.ds(index * cols, cols)
        height = pl.ds(0, capacity if packed else rows)
        into = block
        if not upward:
            target = exp if landing else exp - 1
            into = jnp.where(block == target, experts, block)
        return remote(
            tok.at[block, height, part],
            rx.at[into, height, part],
            ret_send.at[block, index],
            ret_recv.at[into, index],
            up if upward else dn,
        )

    def share(block, at, height=rows):
        part = pl.ds(0, height)
        total = jnp.dot(act[0, block, part], wd[0, :, at], preferred_element_type=jnp.float32)
        for slot in range(1, span):
            total = total + jnp.dot(act[slot, block, part], wd[slot, :, at], preferred_element_type=jnp.float32)
        return total

    def packing(block, expert):
        sublane = lax.broadcasted_iota(jnp.int32, (gates.shape[1], rows), 0)
        row = jnp.sum(jnp.where(sublane == expert, gates[block], 0.0), axis=0, keepdims=True)
        taken = jnp.broadcast_to(jnp.where(row != 0.0, 1.0, 0.0), (capacity, rows))
        source = lax.broadcasted_iota(jnp.int32, (rows, rows), 0)
        dest = lax.broadcasted_iota(jnp.int32, (rows, rows), 1)
        earlier = jnp.where(source < dest, 1.0, 0.0).astype(jnp.bfloat16)
        rank = jnp.dot(taken.astype(jnp.bfloat16), earlier, preferred_element_type=jnp.float32)
        slot = lax.broadcasted_iota(jnp.int32, (capacity, rows), 0).astype(jnp.float32)
        return jnp.where(rank == slot, taken, 0.0).astype(jnp.bfloat16)

    def unpacked(picks, value):
        return lax.dot_general(picks, value, (((0,), (0,)), ((), ())), preferred_element_type=jnp.float32)

    def tiles_of(index, body):
        def run(i, carry):
            body(pl.ds(pl.multiple_of(index * cols + i * tile, tile), tile))
            return carry

        lax.fori_loop(0, cols // tile, run, 0)

    def neighbour(upward):
        return exp - 1 if upward else exp + 1

    def is_end(expert, upward):
        return expert == (0 if upward else last)

    def send_result(block, index, upward):
        first = is_end(exp, upward)
        second = is_end(neighbour(upward), upward)

        @pl.when(first)
        def _():
            if index == 0:
                picks = packing(block, exp)
                for slot in range(span):
                    act[slot, block, pl.ds(0, capacity)] = jnp.dot(
                        picks, act[slot, block], preferred_element_type=jnp.float32
                    ).astype(jnp.bfloat16)

            def body(at):
                tok[block, pl.ds(0, capacity), at] = share(block, at, capacity).astype(jnp.bfloat16)

            tiles_of(index, body)
            out_copy(block, index, upward, False, True).start()

        @pl.when(second)
        def _():
            out_copy(block, index, upward, True, True).wait_recv()
            picks = packing(block, neighbour(upward))

            def body(at):
                total = share(block, at) + unpacked(picks, rx[block, pl.ds(0, capacity), at])
                tok[block, :, at] = total.astype(jnp.bfloat16)

            tiles_of(index, body)

        @pl.when(jnp.logical_not(jnp.logical_or(first, second)))
        def _():
            out_copy(block, index, upward, True, False).wait_recv()

            def body(at):
                total = share(block, at) + rx[block, :, at].astype(jnp.float32)
                tok[block, :, at] = total.astype(jnp.bfloat16)

            tiles_of(index, body)

        @pl.when(jnp.logical_not(first))
        def _():
            out_copy(block, index, upward, False, False).start()

    def return_step(step, carry):
        low = exp - (experts - step)
        high = exp + (experts - step)
        for index in range(OUT_PIECES):

            @pl.when(low >= 0)
            def _():
                send_result(jnp.maximum(low, 0), index, False)

            @pl.when(high <= last)
            def _():
                send_result(jnp.minimum(high, last), index, True)

        return carry

    lax.fori_loop(1, experts, return_step, 0)

    def own_body(i, carry):
        at = pl.ds(pl.multiple_of(i * tile, tile), tile)
        acc[:, at] = res_ref[:, at].astype(jnp.float32) + share(exp, at)
        return carry

    lax.fori_loop(0, width // tile, own_body, 0)

    def join(index, upward):
        slot = exp if upward else experts
        second = is_end(neighbour(upward), upward)

        @pl.when(second)
        def _():
            out_copy(exp, index, upward, True, True).wait_recv()
            picks = packing(exp, neighbour(upward))

            def body(at):
                acc[:, at] += unpacked(picks, rx[slot, pl.ds(0, capacity), at])

            tiles_of(index, body)

        @pl.when(jnp.logical_not(jnp.logical_or(second, is_end(exp, upward))))
        def _():
            out_copy(exp, index, upward, True, False).wait_recv()

            def body(at):
                acc[:, at] += rx[slot, :, at].astype(jnp.float32)

            tiles_of(index, body)

    for index in range(OUT_PIECES):
        join(index, True)
        join(index, False)

        def write(at):
            out_ref[:, at] = acc[:, at].astype(jnp.bfloat16)

        tiles_of(index, write)

    def wait_result(block, upward):
        first = is_end(exp, upward)

        @pl.when(first)
        def _():
            for index in range(OUT_PIECES):
                out_copy(block, index, upward, False, True).wait_send()

        @pl.when(jnp.logical_not(first))
        def _():
            for index in range(OUT_PIECES):
                out_copy(block, index, upward, False, False).wait_send()

    def results_sent(block, carry):
        @pl.when(block < exp)
        def _():
            wait_result(block, False)

        @pl.when(block > exp)
        def _():
            wait_result(block, True)

        return carry

    lax.fori_loop(0, experts, results_sent, 0)
    for mat in range(3):
        c_copy(mat, False).wait_send()
        for index in range(W_PIECES[mat]):
            y_copy(mat, index, False).wait_send()
            cy_copy(mat, index, False).wait_send()
            for i in range(groups - 1):
                x_copy(mat, index, i, False).wait_send()
                cx_copy(mat, index, i, False).wait_send()


def shards(residual, norm_gain, router, w_gate, w_up, w_down, expert_ids):
    rows, width = residual.shape
    experts = router.shape[1]
    groups = lax.axis_size("groups")
    span = lax.axis_size("expert") // experts
    assert span == 4
    hid = w_gate.shape[1]
    capacity = 3 * rows * expert_ids.shape[1] // (2 * experts)
    capacity = min(rows, -(-capacity // 16) * 16)
    vmem = pl.BlockSpec(memory_space=pltpu.VMEM)
    anywhere = pl.BlockSpec(memory_space=pl.ANY)
    dma = pltpu.SemaphoreType.DMA
    weight_copies = sum(W_PIECES)
    return pl.pallas_call(
        functools.partial(kernel, groups, experts, span, capacity),
        out_shape=jax.ShapeDtypeStruct((rows, width), jnp.bfloat16),
        in_specs=[vmem, vmem, vmem, vmem, anywhere, anywhere, anywhere],
        out_specs=vmem,
        scratch_shapes=[
            pltpu.VMEM((experts, rows, width), jnp.bfloat16),
            pltpu.VMEM((experts, experts, rows), jnp.float32),
            pltpu.VMEM((span, experts, rows, hid), jnp.bfloat16),
            pltpu.VMEM((experts + 1, rows, width), jnp.bfloat16),
            pltpu.VMEM((rows, width), jnp.float32),
            pltpu.VMEM((span, width, hid), jnp.bfloat16),
            pltpu.VMEM((span, width, hid), jnp.bfloat16),
            pltpu.VMEM((span, hid, width), jnp.bfloat16),
            dma((3,)),
            dma((experts, TOK_PIECES)),
            dma((experts, TOK_PIECES)),
            dma((experts, TOK_PIECES)),
            dma((experts,)),
            dma((experts,)),
            dma((experts,)),
            dma((experts, OUT_PIECES)),
            dma((experts + 1, OUT_PIECES)),
            dma((weight_copies,)),
            dma((weight_copies,)),
            dma((groups - 1, weight_copies)),
            dma((groups - 1, weight_copies)),
            dma((3,)),
            dma((3,)),
            dma((weight_copies,)),
            dma((weight_copies,)),
            dma((groups - 1, weight_copies)),
            dma((groups - 1, weight_copies)),
        ],
        compiler_params=pltpu.CompilerParams(
            collective_id=0, has_side_effects=True, vmem_limit_bytes=67043328
        ),
    )(residual, norm_gain, router.T, expert_ids.T, w_gate, w_up, w_down)


def solution(mesh):
    in_specs = (
        P(("groups", "expert"), None),
        P(),
        P(),
        P(None, "expert"),
        P(None, "expert"),
        P("expert", None),
        P(("groups", "expert"), None),
    )
    out_specs = P(("groups", "expert"), None)
    return jax.shard_map(shards, mesh=mesh, in_specs=in_specs, out_specs=out_specs, check_vma=False)
```

```python
import functools

import jax
import jax.numpy as jnp
from jax import lax
from jax.experimental import pallas as pl
from jax.experimental.pallas import tpu as pltpu
from jax.sharding import PartitionSpec as P

route_scale = 2.5
norm_eps = 1e-06
LANES = 128
MESH = pl.DeviceIdType.MESH

TOK_PIECES = 2
OUT_PIECES = 7
W_PIECES = (4, 4, 7)


def kernel(
    groups,
    experts,
    span,
    capacity,
    res_ref,
    gain_ref,
    router_ref,
    ids_ref,
    wg_in,
    wu_in,
    wd_in,
    out_ref,
    tok,
    gates,
    act,
    rx,
    acc,
    wg,
    wu,
    wd,
    own_sem,
    tok_recv,
    tok_up,
    tok_dn,
    gate_recv,
    gate_up,
    gate_dn,
    ret_send,
    ret_recv,
    y_send,
    y_recv,
    x_send,
    x_recv,
    c_send,
    c_recv,
    cy_send,
    cy_recv,
    cx_send,
    cx_recv,
):
    rows, width = res_ref.shape
    hid = wg_in.shape[1]
    grp = lax.axis_index("groups")
    pos = lax.axis_index("expert")
    exp = pos // span
    mem = pos % span
    last = experts - 1
    has_up = exp < last
    has_dn = exp > 0
    base = exp * span
    mem_y = (mem + 2) % 4
    mem_c = mem + 1 - 2 * (mem % 2)
    mem_yc = (mem_c + 2) % 4
    up = {"groups": grp, "expert": jnp.minimum(pos + span, experts * span - 1)}
    dn = {"groups": grp, "expert": jnp.maximum(pos - span, 0)}
    to_y = {"groups": grp, "expert": base + mem_y}
    to_c = {"groups": grp, "expert": base + mem_c}

    def other(i):
        return (grp + 1 + i) % groups

    barrier = pltpu.get_barrier_semaphore()

    def greet(device):
        pl.semaphore_signal(barrier, inc=1, device_id=device, device_id_type=MESH)

    greet(to_y)
    greet(to_c)
    for i in range(groups - 1):
        greet({"groups": other(i), "expert": pos})

    @pl.when(has_up)
    def _():
        greet(up)

    @pl.when(has_dn)
    def _():
        greet(dn)

    peers = 1 + groups + has_up.astype(jnp.int32) + has_dn.astype(jnp.int32)
    pl.semaphore_wait(barrier, peers)

    mats = ((wg_in, wg), (wu_in, wu), (wd_in, wd))

    def piece(ref, mat, group, index):
        total = mats[mat][0].shape[mat // 2]
        size = total // groups // W_PIECES[mat]
        part = pl.ds(pl.multiple_of(group * (total // groups) + index * size, size), size)
        return ref.at[:, part] if mat == 2 else ref.at[part]

    def number(mat, index):
        return sum(W_PIECES[:mat]) + index

    def remote(src, dst, send, recv, device):
        return pltpu.make_async_remote_copy(
            src_ref=src, dst_ref=dst, send_sem=send, recv_sem=recv, device_id=device, device_id_type=MESH
        )

    def y_copy(mat, index, landing):
        at = number(mat, index)
        into = piece(mats[mat][1].at[mem_y if landing else mem], mat, grp, index)
        return remote(piece(mats[mat][0], mat, grp, index), into, y_send.at[at], y_recv.at[at], to_y)

    def x_copy(mat, index, i, landing):
        at = number(mat, index)
        group = (grp + groups - 1 - i) % groups if landing else grp
        ref = piece(mats[mat][1].at[mem_y], mat, group, index)
        return remote(ref, ref, x_send.at[i, at], x_recv.at[i, at], {"groups": other(i), "expert": pos})

    def cy_copy(mat, index, landing):
        at = number(mat, index)
        ref = piece(mats[mat][1].at[mem_yc if landing else mem_y], mat, grp, index)
        return remote(ref, ref, cy_send.at[at], cy_recv.at[at], to_c)

    def cx_copy(mat, index, i, landing):
        at = number(mat, index)
        group = (grp + groups - 1 - i) % groups
        ref = piece(mats[mat][1].at[mem_yc if landing else mem_y], mat, group, index)
        return remote(ref, ref, cx_send.at[i, at], cx_recv.at[i, at], to_c)

    def c_copy(mat, landing):
        slot = mem_c if landing else mem
        return remote(mats[mat][0], mats[mat][1].at[slot], c_send.at[mat], c_recv.at[mat], to_c)

    for mat in range(3):
        for index in range(W_PIECES[mat]):
            y_copy(mat, index, False).start()
    own_copies = [pltpu.make_async_copy(mats[i][0], mats[i][1].at[mem], own_sem.at[i]) for i in range(3)]
    for mat in range(3):
        c_copy(mat, False).start()
        own_copies[mat].start()

    step_rows = 16

    def norm_rows(i, carry):
        at = pl.ds(pl.multiple_of(i * step_rows, step_rows), step_rows)
        wide = res_ref[at, :].astype(jnp.float32)
        mean = jnp.mean(wide * wide, axis=1, keepdims=True)
        tok[exp, at, :] = (wide * lax.rsqrt(mean + norm_eps) * gain_ref[...].reshape(1, width)).astype(jnp.bfloat16)
        return carry

    piece_rows = rows // TOK_PIECES

    def tok_copy(block, index, upward):
        ref = tok.at[block, pl.ds(index * piece_rows, piece_rows)]
        send = (tok_up if upward else tok_dn).at[block, index]
        return remote(ref, ref, send, tok_recv.at[block, index], up if upward else dn)

    def gate_copy(block, upward):
        ref = gates.at[block]
        send = (gate_up if upward else gate_dn).at[block]
        return remote(ref, ref, send, gate_recv.at[block], up if upward else dn)

    def send_block(block, index, upward):
        tok_copy(block, index, upward).start()
        if index == TOK_PIECES - 1:
            gate_copy(block, upward).start()

    def gate_values():
        logits = lax.dot_general(
            router_ref[...], tok[exp], (((1,), (1,)), ((), ())), preferred_element_type=jnp.float32
        )
        affinity = jax.nn.sigmoid(logits)
        expert = lax.broadcasted_iota(jnp.int32, (experts, rows), 0)
        spread = jnp.zeros((experts, rows), jnp.float32)
        for k in range(ids_ref.shape[0]):
            spread = spread + jnp.where(expert == ids_ref[k : k + 1, :], affinity, 0.0)
        gates[exp] = route_scale * spread / jnp.sum(spread, axis=0, keepdims=True)

    steps = piece_rows // step_rows
    for index in range(TOK_PIECES):
        lax.fori_loop(index * steps, (index + 1) * steps, norm_rows, 0)

        @pl.when(has_up)
        def _():
            tok_copy(exp, index, True).start()

        @pl.when(has_dn)
        def _():
            tok_copy(exp, index, False).start()

    gate_values()

    @pl.when(has_up)
    def _():
        gate_copy(exp, True).start()

    @pl.when(has_dn)
    def _():
        gate_copy(exp, False).start()

    def weight_tick(mat, index):
        y_copy(mat, index, True).wait_recv()
        for i in range(groups - 1):
            x_copy(mat, index, i, False).start()
        cy_copy(mat, index, False).start()

    def weight_late(mat, index):
        for i in range(groups - 1):
            x_copy(mat, index, i, True).wait_recv()
            cx_copy(mat, index, i, False).start()

    def token_tick(step, index):
        low = exp - step
        high = exp + step

        @pl.when(low >= 0)
        def _():
            tok_copy(jnp.maximum(low, 0), index, True).wait_recv()
            if index == TOK_PIECES - 1:
                gate_copy(jnp.maximum(low, 0), True).wait_recv()

        @pl.when(jnp.logical_and(low >= 0, has_up))
        def _():
            send_block(jnp.maximum(low, 0), index, True)

        @pl.when(high <= last)
        def _():
            tok_copy(jnp.minimum(high, last), index, False).wait_recv()
            if index == TOK_PIECES - 1:
                gate_copy(jnp.minimum(high, last), False).wait_recv()

        @pl.when(jnp.logical_and(high <= last, has_dn))
        def _():
            send_block(jnp.minimum(high, last), index, False)

    def hidden_part(block, slot):
        rows_in = tok[block]
        gate_proj = jnp.dot(rows_in, wg[slot], preferred_element_type=jnp.float32)
        up_proj = jnp.dot(rows_in, wu[slot], preferred_element_type=jnp.float32)
        sublane = lax.broadcasted_iota(jnp.int32, (gates.shape[1], rows), 0)
        row = jnp.sum(jnp.where(sublane == exp, gates[block], 0.0), axis=0, keepdims=True)
        scale = jnp.broadcast_to(row, (LANES, rows)).T[:, :1]
        hidden = gate_proj / (1.0 + jnp.exp(-gate_proj)) * up_proj * scale
        act[slot, block] = hidden.astype(jnp.bfloat16)

    def first_slices():
        for mat in range(2):
            own_copies[mat].wait()
            c_copy(mat, True).wait_recv()

    def all_slices():
        for mat in range(2):
            for index in range(W_PIECES[mat]):
                cy_copy(mat, index, True).wait_recv()
                for i in range(groups - 1):
                    cx_copy(mat, index, i, True).wait_recv()

    def hidden_step(step, first, second, count=2):
        def body(i, carry):
            side = i // count
            turn = i % count
            block = exp - step + 2 * step * side
            slot = jnp.where(turn == 0, first, jnp.where(turn == 1, second, jnp.where(turn == 2, mem_y, mem_yc)))

            @pl.when(jnp.logical_and(block >= 0, block <= last))
            def _():
                hidden_part(jnp.clip(block, 0, last), slot)

            return carry

        lax.fori_loop(0, count if step == 0 else 2 * count, body, 0)

    events = []
    for mat in range(3):
        for index in range(W_PIECES[mat]):
            size = 1 / 3 / W_PIECES[mat]
            when = mat / 3 + (index + 1) * size
            events.append((when, 0, functools.partial(weight_tick, mat, index)))
            events.append((when + size, 1, functools.partial(weight_late, mat, index)))
    token_steps = last * TOK_PIECES
    for tick in range(token_steps):
        step, index = divmod(tick, TOK_PIECES)
        events.append(((tick + 1) / token_steps, 2, functools.partial(token_tick, step + 1, index)))
    ready = 0.83
    events.append((0.12, 3, first_slices))
    events.append((ready, 3, all_slices))
    for step in range(experts):
        there = max(step / last, 0.12)
        if step == last and last >= 2:
            continue
        if there >= ready:
            events.append((there, 4, functools.partial(hidden_step, step, mem, mem_c, span)))
        else:
            events.append((there, 4, functools.partial(hidden_step, step, mem, mem_c)))
            late = ready + 0.04 * step
            events.append((late, 4, functools.partial(hidden_step, step, mem_y, mem_yc)))
    events.sort(key=lambda event: event[:2])
    for event in events:
        event[2]()

    own_copies[2].wait()
    c_copy(2, True).wait_recv()
    for index in range(W_PIECES[2]):
        cy_copy(2, index, True).wait_recv()
        for i in range(groups - 1):
            cx_copy(2, index, i, True).wait_recv()

    def sent(block, carry):
        @pl.when(jnp.logical_and(block <= exp, has_up))
        def _():
            for index in range(TOK_PIECES):
                tok_copy(block, index, True).wait_send()
            gate_copy(block, True).wait_send()

        @pl.when(jnp.logical_and(block >= exp, has_dn))
        def _():
            for index in range(TOK_PIECES):
                tok_copy(block, index, False).wait_send()
            gate_copy(block, False).wait_send()

        return carry

    lax.fori_loop(0, experts, sent, 0)

    cols = width // OUT_PIECES
    tile = 256

    def out_copy(block, index, upward, landing, packed):
        part = pl.ds(pl.multiple_of(index * cols, cols), cols)
        height = pl.ds(0, capacity if packed else rows)
        into = block
        if not upward:
            target = exp if landing else exp - 1
            into = jnp.where(block == target, experts, block)
        return remote(
            tok.at[block, height, part],
            rx.at[into, height, part],
            ret_send.at[block, index],
            ret_recv.at[into, index],
            up if upward else dn,
        )

    def share(block, at, height=rows):
        part = pl.ds(0, height)
        total = jnp.dot(act[0, block, part], wd[0, :, at], preferred_element_type=jnp.float32)
        for slot in range(1, span):
            total = total + jnp.dot(act[slot, block, part], wd[slot, :, at], preferred_element_type=jnp.float32)
        return total

    def packing(block, expert):
        sublane = lax.broadcasted_iota(jnp.int32, (gates.shape[1], rows), 0)
        row = jnp.sum(jnp.where(sublane == expert, gates[block], 0.0), axis=0, keepdims=True)
        taken = jnp.broadcast_to(jnp.where(row != 0.0, 1.0, 0.0), (capacity, rows))
        source = lax.broadcasted_iota(jnp.int32, (rows, rows), 0)
        dest = lax.broadcasted_iota(jnp.int32, (rows, rows), 1)
        earlier = jnp.where(source < dest, 1.0, 0.0).astype(jnp.bfloat16)
        rank = jnp.dot(taken.astype(jnp.bfloat16), earlier, preferred_element_type=jnp.float32)
        slot = lax.broadcasted_iota(jnp.int32, (capacity, rows), 0).astype(jnp.float32)
        return jnp.where(rank == slot, taken, 0.0).astype(jnp.bfloat16)

    def unpacked(picks, value):
        return lax.dot_general(picks, value, (((0,), (0,)), ((), ())), preferred_element_type=jnp.float32)

    def tiles_of(index, body):
        def run(i, carry):
            body(pl.ds(pl.multiple_of(index * cols + i * tile, tile), tile))
            return carry

        lax.fori_loop(0, cols // tile, run, 0)

    def neighbour(upward):
        return exp - 1 if upward else exp + 1

    def is_end(expert, upward):
        return expert == (0 if upward else last)

    def send_result(block, index, upward):
        first = is_end(exp, upward)
        second = is_end(neighbour(upward), upward)

        @pl.when(first)
        def _():
            @pl.when(index == 0)
            def _():
                picks = packing(block, exp)
                for slot in range(span):
                    act[slot, block, pl.ds(0, capacity)] = jnp.dot(
                        picks, act[slot, block], preferred_element_type=jnp.float32
                    ).astype(jnp.bfloat16)

            def body(at):
                tok[block, pl.ds(0, capacity), at] = share(block, at, capacity).astype(jnp.bfloat16)

            tiles_of(index, body)
            out_copy(block, index, upward, False, True).start()

        @pl.when(second)
        def _():
            out_copy(block, index, upward, True, True).wait_recv()
            picks = packing(block, neighbour(upward))

            def body(at):
                total = share(block, at) + unpacked(picks, rx[block, pl.ds(0, capacity), at])
                tok[block, :, at] = total.astype(jnp.bfloat16)

            tiles_of(index, body)

        @pl.when(jnp.logical_not(jnp.logical_or(first, second)))
        def _():
            out_copy(block, index, upward, True, False).wait_recv()

            def body(at):
                total = share(block, at) + rx[block, :, at].astype(jnp.float32)
                tok[block, :, at] = total.astype(jnp.bfloat16)

            tiles_of(index, body)

        @pl.when(jnp.logical_not(first))
        def _():
            out_copy(block, index, upward, False, False).start()

    ahead = 4
    upper = 2 * exp >= experts

    def swapped(block, reach):
        return jnp.where(jnp.logical_and(reach >= 2, jnp.logical_and(block >= 0, block <= 1)), 1 - block, block)

    def return_step(step, carry):
        if last >= 2:

            @pl.when(step == 2)
            def _():
                hidden_step(last, mem, mem_c, span)

        low = swapped(exp - (experts - step), exp)
        high = last - swapped(last - exp - (experts - step), last - exp)

        def turn(t, inner):
            low_at = jnp.where(upper, t, t - ahead)
            high_at = jnp.where(upper, t - ahead, t)

            @pl.when(jnp.logical_and(low >= 0, jnp.logical_and(low_at >= 0, low_at < OUT_PIECES)))
            def _():
                send_result(jnp.maximum(low, 0), jnp.clip(low_at, 0, OUT_PIECES - 1), False)

            @pl.when(jnp.logical_and(high <= last, jnp.logical_and(high_at >= 0, high_at < OUT_PIECES)))
            def _():
                send_result(jnp.minimum(high, last), jnp.clip(high_at, 0, OUT_PIECES - 1), True)

            return inner

        lax.fori_loop(0, OUT_PIECES + ahead, turn, 0)
        return carry

    lax.fori_loop(1, experts, return_step, 0)

    def own_body(i, carry):
        at = pl.ds(pl.multiple_of(i * tile, tile), tile)
        acc[:, at] = res_ref[:, at].astype(jnp.float32) + share(exp, at)
        return carry

    lax.fori_loop(0, width // tile, own_body, 0)

    def join(index, upward):
        slot = exp if upward else experts
        second = is_end(neighbour(upward), upward)

        @pl.when(second)
        def _():
            out_copy(exp, index, upward, True, True).wait_recv()
            picks = packing(exp, neighbour(upward))

            def body(at):
                acc[:, at] += unpacked(picks, rx[slot, pl.ds(0, capacity), at])

            tiles_of(index, body)

        @pl.when(jnp.logical_not(jnp.logical_or(second, is_end(exp, upward))))
        def _():
            out_copy(exp, index, upward, True, False).wait_recv()

            def body(at):
                acc[:, at] += rx[slot, :, at].astype(jnp.float32)

            tiles_of(index, body)

    for index in range(OUT_PIECES):
        join(index, True)
        join(index, False)

        def write(at):
            out_ref[:, at] = acc[:, at].astype(jnp.bfloat16)

        tiles_of(index, write)

    def wait_result(block, upward):
        first = is_end(exp, upward)

        @pl.when(first)
        def _():
            for index in range(OUT_PIECES):
                out_copy(block, index, upward, False, True).wait_send()

        @pl.when(jnp.logical_not(first))
        def _():
            for index in range(OUT_PIECES):
                out_copy(block, index, upward, False, False).wait_send()

    def results_sent(block, carry):
        @pl.when(block < exp)
        def _():
            wait_result(block, False)

        @pl.when(block > exp)
        def _():
            wait_result(block, True)

        return carry

    lax.fori_loop(0, experts, results_sent, 0)
    for mat in range(3):
        c_copy(mat, False).wait_send()
        for index in range(W_PIECES[mat]):
            y_copy(mat, index, False).wait_send()
            cy_copy(mat, index, False).wait_send()
            for i in range(groups - 1):
                x_copy(mat, index, i, False).wait_send()
                cx_copy(mat, index, i, False).wait_send()


def shards(residual, norm_gain, router, w_gate, w_up, w_down, expert_ids):
    rows, width = residual.shape
    experts = router.shape[1]
    groups = lax.axis_size("groups")
    span = lax.axis_size("expert") // experts
    assert span == 4
    hid = w_gate.shape[1]
    capacity = 3 * rows * expert_ids.shape[1] // (2 * experts)
    capacity = min(rows, -(-capacity // 16) * 16)
    vmem = pl.BlockSpec(memory_space=pltpu.VMEM)
    anywhere = pl.BlockSpec(memory_space=pl.ANY)
    dma = pltpu.SemaphoreType.DMA
    weight_copies = sum(W_PIECES)
    return pl.pallas_call(
        functools.partial(kernel, groups, experts, span, capacity),
        out_shape=jax.ShapeDtypeStruct((rows, width), jnp.bfloat16),
        in_specs=[vmem, vmem, vmem, vmem, anywhere, anywhere, anywhere],
        out_specs=vmem,
        scratch_shapes=[
            pltpu.VMEM((experts, rows, width), jnp.bfloat16),
            pltpu.VMEM((experts, experts, rows), jnp.float32),
            pltpu.VMEM((span, experts, rows, hid), jnp.bfloat16),
            pltpu.VMEM((experts + 1, rows, width), jnp.bfloat16),
            pltpu.VMEM((rows, width), jnp.float32),
            pltpu.VMEM((span, width, hid), jnp.bfloat16),
            pltpu.VMEM((span, width, hid), jnp.bfloat16),
            pltpu.VMEM((span, hid, width), jnp.bfloat16),
            dma((3,)),
            dma((experts, TOK_PIECES)),
            dma((experts, TOK_PIECES)),
            dma((experts, TOK_PIECES)),
            dma((experts,)),
            dma((experts,)),
            dma((experts,)),
            dma((experts, OUT_PIECES)),
            dma((experts + 1, OUT_PIECES)),
            dma((weight_copies,)),
            dma((weight_copies,)),
            dma((groups - 1, weight_copies)),
            dma((groups - 1, weight_copies)),
            dma((3,)),
            dma((3,)),
            dma((weight_copies,)),
            dma((weight_copies,)),
            dma((groups - 1, weight_copies)),
            dma((groups - 1, weight_copies)),
        ],
        compiler_params=pltpu.CompilerParams(
            collective_id=0, has_side_effects=True, vmem_limit_bytes=67043328
        ),
    )(residual, norm_gain, router.T, expert_ids.T, w_gate, w_up, w_down)


def solution(mesh):
    in_specs = (
        P(("groups", "expert"), None),
        P(),
        P(),
        P(None, "expert"),
        P(None, "expert"),
        P("expert", None),
        P(("groups", "expert"), None),
    )
    out_specs = P(("groups", "expert"), None)
    return jax.shard_map(shards, mesh=mesh, in_specs=in_specs, out_specs=out_specs, check_vma=False)
```
